32 devices in a mesh: groups: 2 (over y), feat: 4 (over z), rows: 2 (over x), sub: 2 (over core).
Axes of the slice: x: 2, y: 2, z: 4, core: 2. Of those that a mesh axis runs over, the one named last changes fastest.
Arguments:
- acts: bfloat16 [256, 32, 8192], P(('groups', 'rows', 'sub'), None, 'feat'), parts along dimension 0, may hold values from -6 to 6
- out_grads: bfloat16 [256, 32, 8192], P(('groups', 'rows', 'sub'), None, 'feat'), parts along dimension 0, may hold values from -6 to 6
- proj_in: bfloat16 [8192, 128], P('feat'), may hold values from -0.0625 to 0.0625
- proj_out: bfloat16 [8192, 128], P('feat'), may hold values from -0.0625 to 0.0625
- store: float32 [5120, 16384], P(('groups', 'rows', 'sub'), 'feat'), parts along dimension 0, may hold values from -0.0084 to 0.0084
Outputs:
- scores: float32 [256, 2560], P(('groups', 'feat'), ('rows', 'sub')), parts along dimension 0
The draws below stay inside these ranges and needn't reach their ends.
There are 2 independent parts, one for each index of `groups`. The reference program is written for one: setup_inputs(seed, part) draws one part's arguments, and reference() takes and returns one part's arrays. A program takes and returns all parts, laid end to end along the dimension named above; an argument that names none is the same for every part. Nothing has to cross between parts.
All inputs are finite; a program needn't handle non-finite values.
Results may differ from the reference program's by a relative error of at most 0.0003.
Values sent between devices are 32-bit elements; how exact they have to be, the bound alone decides.
A program may use at most 64 MiB of HBM per device.

```python
import jax
import jax.numpy as jnp
from jax import lax

D = 8192
RANK = 128
TOK = 32
FEATS = 16384
QUERIES = 128
EXAMPLES = 2560


def steps_of(rng, extent, shards, least, largest):
    factor_of = 1.0
    for position, shards_of in shards:
        heights = jax.random.uniform(jax.random.fold_in(jax.random.fold_in(rng, 6), position), (shards_of,), jnp.float32, least / len(shards), largest / len(shards))
        factor_of = factor_of * jnp.repeat(jnp.exp(heights), extent[position] // shards_of).reshape((-1,) + (1,) * (len(extent) - 1 - position))
    return factor_of


def centred(rng, extent, spread, reach, cuts=(), kind=jnp.bfloat16):
    values = spread * jax.random.normal(rng, extent, jnp.float32)
    if cuts:
        values = values * steps_of(rng, extent, cuts, -0.22, 0.18)
    return jnp.clip(values, -reach, reach).astype(kind)


def setup_inputs(seed: int = 0, part: int = 0) -> dict:
    keys = jax.random.split(jax.random.key(seed), 6)
    part_splits = jax.random.split(jax.random.fold_in(keys[5], part), 6)
    acts = centred(part_splits[0], (QUERIES, TOK, D), 1.0, 6.0, ((0, 4), (2, 4)))
    out_grads = centred(part_splits[1], (QUERIES, TOK, D), 1.0, 6.0, ((0, 4), (2, 4)))
    proj_in = centred(keys[2], (D, RANK), D ** -0.5, 0.0625, ((0, 4),))
    proj_out = centred(keys[3], (D, RANK), D ** -0.5, 0.0625, ((0, 4),))
    store = centred(part_splits[4], (EXAMPLES, FEATS), 0.0014, 0.0084, ((0, 4), (1, 4)), jnp.float32)
    return {"acts": acts, "out_grads": out_grads, "proj_in": proj_in, "proj_out": proj_out, "store": store}


def reference(acts, out_grads, proj_in, proj_out, store):
    flat_acts = acts.reshape(QUERIES * TOK, D)
    flat_grads = out_grads.reshape(QUERIES * TOK, D)
    in_proj = jnp.dot(flat_acts, proj_in, preferred_element_type=jnp.float32).reshape(QUERIES, TOK, RANK)
    out_proj = jnp.dot(flat_grads, proj_out, preferred_element_type=jnp.float32).reshape(QUERIES, TOK, RANK)
    query_grad = jnp.einsum("qti,qtj->qij", out_proj.astype(jnp.float32), in_proj.astype(jnp.float32), precision=lax.Precision.HIGHEST).reshape(QUERIES, RANK * RANK)
    scores = lax.dot_general(query_grad, store, (((1,), (1,)), ((), ())), precision=lax.Precision.HIGHEST, preferred_element_type=jnp.float32)
    return scores
```

```python
import functools

import jax
import jax.numpy as jnp
from jax import lax
from jax.experimental import pallas as pl
from jax.experimental.pallas import tpu as pltpu
from jax.sharding import PartitionSpec as P

MESH = pl.DeviceIdType.MESH
LANES = 128
F32 = jnp.float32
BF16 = jnp.bfloat16
LAG = 2


def split(x):
    hi = x.astype(BF16)
    return hi, (x - hi.astype(F32)).astype(BF16)


def dot_nt(a, b):
    return lax.dot_general(a, b, (((1,), (1,)), ((), ())), preferred_element_type=F32)


def kernel(
    n, rows, subs, tokens,
    acts, grads, pin, pout, store, out,
    xa, xg, st, shi, slo, own, ups, upr, dns, dnr, tsum, gbuf, glhs, sbuf, rbuf,
    load_sem, z_send, z_recv, x_send, x_recv, c_send, c_recv, f_send, f_recv, s_send, s_recv,
):
    f = lax.axis_index("feat")
    row = lax.axis_index("rows")
    sub = lax.axis_index("sub")
    chunks, tok, _ = xa.shape
    rank = pin.shape[1]
    shard = rank // n
    per = tok // tokens
    here = chunks * per
    total = here * rows * subs
    piece = store.shape[0] // chunks
    mine = total // n
    blocks = sbuf.shape[0]

    def load(kind, c):
        src, dst, size = ((acts, xa, tok), (grads, xg, tok), (store, st, piece))[kind]
        return pltpu.make_async_copy(
            src.at[pl.ds(pl.multiple_of(c * size, size), size)], dst.at[c], load_sem.at[kind, c]
        )

    for c in range(chunks):
        load(0, c).start()
        load(1, c).start()
    for c in range(chunks):
        load(2, c).start()

    barrier = pltpu.get_barrier_semaphore()
    for o in range(1, n):
        pl.semaphore_signal(barrier, device_id={"feat": lax.rem(f + o, n)}, device_id_type=MESH)
    for o in range(1, rows):
        pl.semaphore_signal(barrier, device_id={"rows": lax.rem(row + o, rows)}, device_id_type=MESH)
    for o in range(1, subs):
        pl.semaphore_signal(barrier, device_id={"sub": lax.rem(sub + o, subs)}, device_id_type=MESH)
    pl.semaphore_wait(barrier, n + rows + subs - 3)

    def up(c):
        return pltpu.make_async_remote_copy(
            ups.at[c], upr.at[c], z_send.at[0, c], z_recv.at[0, c],
            device_id={"feat": lax.rem(f + 1, n)}, device_id_type=MESH)

    def down(c):
        return pltpu.make_async_remote_copy(
            dns.at[c], dnr.at[c], z_send.at[1, c], z_recv.at[1, c],
            device_id={"feat": lax.rem(f + n - 1, n)}, device_id_type=MESH)

    def slot(r, s, c):
        size = per * shard
        return gbuf.at[pl.ds(pl.multiple_of(((r * subs + s) * chunks + c) * size, size), size)]

    def across(o, c):
        ref = slot(row, sub, c)
        return pltpu.make_async_remote_copy(
            ref, ref, x_send.at[o - 1, c], x_recv.at[o - 1, c],
            device_id={"rows": lax.rem(row + o, rows)}, device_id_type=MESH)

    def beside(o, c):
        ref = slot(row, sub, c)
        return pltpu.make_async_remote_copy(
            ref, ref, c_send.at[o - 1, c], c_recv.at[o - 1, c],
            device_id={"sub": lax.rem(sub + o, subs)}, device_id_type=MESH)

    def onward(o, p, c):
        ref = slot(lax.rem(row + rows - o, rows), sub, c)
        k = (o - 1) * (subs - 1) + p - 1
        return pltpu.make_async_remote_copy(
            ref, ref, f_send.at[k, c], f_recv.at[k, c],
            device_id={"sub": lax.rem(sub + p, subs)}, device_id_type=MESH)

    def step(s, carry):
        @pl.when(s < chunks)
        def _():
            load(0, s).wait()
            load(1, s).wait()
            a = jnp.dot(xa[s], pin[...], preferred_element_type=F32)
            b = jnp.dot(xg[s], pout[...], preferred_element_type=F32)
            own[s, pl.ds(0, rank), :] = b.T
            own[s, pl.ds(rank, tok), :] = a

        cu = s - f

        @pl.when((cu >= 0) & (cu < chunks))
        def _():
            @pl.when(f > 0)
            def _():
                up(cu).wait_recv()

            @pl.when((f > 0) & (f < n - 1))
            def _():
                ups[cu] = own[cu] + upr[cu]

            @pl.when(f == 0)
            def _():
                ups[cu] = own[cu]

            @pl.when(f < n - 1)
            def _():
                up(cu).start()

        cd = s - (n - 1 - f)

        @pl.when((cd >= 0) & (cd < chunks))
        def _():
            @pl.when(f < n - 1)
            def _():
                down(cd).wait_recv()

            @pl.when((f > 0) & (f < n - 1))
            def _():
                dns[cd] = own[cd] + dnr[cd]

            @pl.when(f == n - 1)
            def _():
                dns[cd] = own[cd]

            @pl.when(f > 0)
            def _():
                down(cd).start()

        c = s - jnp.maximum(f, n - 1 - f)

        @pl.when((c >= 0) & (c < chunks))
        def _():
            tsum[...] = own[c]

            @pl.when(f > 0)
            def _():
                tsum[...] += upr[c]

            @pl.when(f < n - 1)
            def _():
                tsum[...] += dnr[c]

            full_in = tsum[pl.ds(rank, tok), :]
            full_out = tsum[pl.ds(pl.multiple_of(f * shard, shard), shard), :]
            lane = lax.broadcasted_iota(jnp.int32, (shard, tok), 1) // tokens
            wide = jnp.concatenate(
                [jnp.where(lane == q, full_out, 0.0) for q in range(per)], axis=0
            )
            g = lax.dot_general(
                wide, full_in, (((1,), (0,)), ((), ())),
                precision=lax.Precision.HIGHEST, preferred_element_type=F32,
            )
            slot(row, sub, c)[...] = g
            for o in range(1, rows):
                across(o, c).start()
            for o in range(1, subs):
                beside(o, c).start()

        late = c - LAG

        @pl.when((late >= 0) & (late < chunks))
        def _():
            for o in range(1, rows):
                across(o, late).wait_recv()
                for p in range(1, subs):
                    onward(o, p, late).start()

        part = s - LAG

        @pl.when((part >= 0) & (part < chunks))
        def _():
            load(2, part).wait()
            hi, lo = split(st[part])
            at = pl.ds(pl.multiple_of(part * piece, piece), piece)
            shi[at, :] = hi
            slo[at, :] = lo

        return carry

    lax.fori_loop(0, chunks + n - 1 + LAG, step, 0)

    def settle(c, carry):
        @pl.when(f < n - 1)
        def _():
            up(c).wait_send()

        @pl.when(f > 0)
        def _():
            down(c).wait_send()

        for o in range(1, rows):
            across(o, c).wait_send()
        for o in range(1, subs):
            beside(o, c).wait()
        for o in range(1, rows):
            for p in range(1, subs):
                onward(o, p, c).wait()
        return carry

    lax.fori_loop(0, chunks, settle, 0)

    def arrange(r, carry):
        for i in range(shard):
            x = gbuf[pl.ds(r * here * shard + i, here, stride=shard), :]
            hi, lo = split(x)
            at = pl.multiple_of(r * here, here)
            glhs[pl.ds(at, here), pl.ds(i * rank, rank)] = hi
            glhs[pl.ds(total + at, here), pl.ds(i * rank, rank)] = lo
        return carry

    lax.fori_loop(0, rows * subs, arrange, 0)

    def send_scores(o, b):
        peer = lax.rem(f + o, n)
        return pltpu.make_async_remote_copy(
            sbuf.at[b, pl.ds(pl.multiple_of(peer * mine, mine), mine)], rbuf.at[o - 1, b],
            s_send.at[o - 1, b], s_recv.at[o - 1, b],
            device_id={"feat": peer}, device_id_type=MESH)

    def score(b, carry):
        at = pl.ds(pl.multiple_of(b * LANES, LANES), LANES)
        both = dot_nt(glhs[...], shi[at, :])
        cross = dot_nt(glhs[pl.ds(0, total), :], slo[at, :])
        sbuf[b] = both[:total] + (both[total:] + cross)
        for o in range(1, n):
            send_scores(o, b).start()
        return carry

    lax.fori_loop(0, blocks, score, 0)

    for b in range(blocks):
        acc = sbuf[b, pl.ds(pl.multiple_of(f * mine, mine), mine), :]
        for o in range(1, n):
            send_scores(o, b).wait_recv()
            acc = acc + rbuf[o - 1, b]
        out[:, pl.ds(b * LANES, LANES)] = acc
    for b in range(blocks):
        for o in range(1, n):
            send_scores(o, b).wait_send()


def local(n, rows, subs, acts, out_grads, proj_in, proj_out, store):
    queries, tokens, width = acts.shape
    rank = proj_in.shape[1]
    examples, feats = store.shape
    tok = LANES
    chunks = queries * tokens // tok
    shard = rank // n
    total = queries * rows * subs
    mine = total // n
    blocks = examples // LANES
    dma = pltpu.SemaphoreType.DMA
    line = pltpu.VMEM((chunks, rank + tok, rank), F32)
    vmem = pl.BlockSpec(memory_space=pltpu.VMEM)
    hbm = pl.BlockSpec(memory_space=pl.ANY)
    hops = (rows - 1) * (subs - 1)
    return pl.pallas_call(
        functools.partial(kernel, n, rows, subs, tokens),
        out_shape=jax.ShapeDtypeStruct((mine, examples), F32),
        in_specs=[hbm, hbm, vmem, vmem, hbm],
        out_specs=vmem,
        scratch_shapes=[
            pltpu.VMEM((chunks, tok, width), BF16),
            pltpu.VMEM((chunks, tok, width), BF16),
            pltpu.VMEM((chunks, examples // chunks, feats), F32),
            pltpu.VMEM((examples, feats), BF16),
            pltpu.VMEM((examples, feats), BF16),
            line, line, line, line, line,
            pltpu.VMEM((rank + tok, rank), F32),
            pltpu.VMEM((total * shard, rank), F32),
            pltpu.VMEM((2 * total, feats), BF16),
            pltpu.VMEM((blocks, total, LANES), F32),
            pltpu.VMEM((n - 1, blocks, mine, LANES), F32),
            dma((3, chunks)),
            dma((2, chunks)), dma((2, chunks)),
            dma((rows - 1, chunks)), dma((rows - 1, chunks)),
            dma((subs - 1, chunks)), dma((subs - 1, chunks)),
            dma((hops, chunks)), dma((hops, chunks)),
            dma((n - 1, blocks)), dma((n - 1, blocks)),
        ],
        compiler_params=pltpu.CompilerParams(
            collective_id=0, has_side_effects=True, vmem_limit_bytes=62 << 20
        ),
    )(
        acts.reshape(queries * tokens, width),
        out_grads.reshape(queries * tokens, width),
        proj_in, proj_out, store,
    )


def solution(mesh):
    n, rows, subs = (mesh.shape[a] for a in ("feat", "rows", "sub"))
    return jax.shard_map(
        functools.partial(local, n, rows, subs),
        mesh=mesh,
        in_specs=(
            P(("groups", "rows", "sub"), None, "feat"),
            P(("groups", "rows", "sub"), None, "feat"),
            P("feat", None),
            P("feat", None),
            P(("groups", "rows", "sub"), "feat"),
        ),
        out_specs=P(("groups", "feat"), ("rows", "sub")),
        check_vma=False,
    )
```

```python
import functools

import jax
import jax.numpy as jnp
from jax import lax
from jax.experimental import pallas as pl
from jax.experimental.pallas import tpu as pltpu
from jax.sharding import PartitionSpec as P

MESH = pl.DeviceIdType.MESH
LANES = 128
F32 = jnp.float32
BF16 = jnp.bfloat16
LAG = 2
SKEW = 2


def split(x):
    hi = x.astype(BF16)
    return hi, (x - hi.astype(F32)).astype(BF16)


def dot_nt(a, b):
    return lax.dot_general(a, b, (((1,), (1,)), ((), ())), preferred_element_type=F32)


def kernel(
    n, rows, subs, tokens,
    acts, grads, pin, pout, store, out,
    xa, xg, st, shi, slo, own, ups, upr, dns, dnr, tsum, gbuf, glhs, sbuf, rbuf,
    load_sem, z_send, z_recv, x_send, x_recv, c_send, c_recv, f_send, f_recv, s_send, s_recv,
):
    f = lax.axis_index("feat")
    row = lax.axis_index("rows")
    sub = lax.axis_index("sub")
    chunks, tok, _ = xa.shape
    rank = pin.shape[1]
    shard = rank // n
    per = tok // tokens
    here = chunks * per
    total = here * rows * subs
    piece = store.shape[0] // chunks
    mine = total // n
    blocks = sbuf.shape[0]

    def load(kind, c):
        src, dst, size = ((acts, xa, tok), (grads, xg, tok), (store, st, piece))[kind]
        return pltpu.make_async_copy(
            src.at[pl.ds(pl.multiple_of(c * size, size), size)], dst.at[c], load_sem.at[kind, c]
        )

    for c in range(chunks):
        load(0, c).start()
        load(1, c).start()
    for c in range(chunks):
        load(2, c).start()

    barrier = pltpu.get_barrier_semaphore()
    for o in range(1, n):
        pl.semaphore_signal(barrier, device_id={"feat": lax.rem(f + o, n)}, device_id_type=MESH)
    for o in range(1, rows):
        pl.semaphore_signal(barrier, device_id={"rows": lax.rem(row + o, rows)}, device_id_type=MESH)
    for o in range(1, subs):
        pl.semaphore_signal(barrier, device_id={"sub": lax.rem(sub + o, subs)}, device_id_type=MESH)
    pl.semaphore_wait(barrier, n + rows + subs - 3)

    def up(k, c):
        at = pl.ds((k + 1) * shard, rank + tok - (k + 1) * shard)
        return pltpu.make_async_remote_copy(
            ups.at[c, at], upr.at[c, at], z_send.at[0, c], z_recv.at[0, c],
            device_id={"feat": lax.rem(f + 1, n)}, device_id_type=MESH)

    def down(k, c):
        at = pl.ds(0, tok + k * shard)
        return pltpu.make_async_remote_copy(
            dns.at[c, at], dnr.at[c, at], z_send.at[1, c], z_recv.at[1, c],
            device_id={"feat": lax.rem(f + n - 1, n)}, device_id_type=MESH)

    def slot(r, s, c):
        size = per * shard
        return gbuf.at[pl.ds(pl.multiple_of(((r * subs + s) * chunks + c) * size, size), size)]

    def across(o, c):
        ref = slot(row, sub, c)
        return pltpu.make_async_remote_copy(
            ref, ref, x_send.at[o - 1, c], x_recv.at[o - 1, c],
            device_id={"rows": lax.rem(row + o, rows)}, device_id_type=MESH)

    def beside(o, c):
        ref = slot(row, sub, c)
        return pltpu.make_async_remote_copy(
            ref, ref, c_send.at[o - 1, c], c_recv.at[o - 1, c],
            device_id={"sub": lax.rem(sub + o, subs)}, device_id_type=MESH)

    def onward(o, p, c):
        ref = slot(lax.rem(row + rows - o, rows), sub, c)
        k = (o - 1) * (subs - 1) + p - 1
        return pltpu.make_async_remote_copy(
            ref, ref, f_send.at[k, c], f_recv.at[k, c],
            device_id={"sub": lax.rem(sub + p, subs)}, device_id_type=MESH)

    def step(s, carry):
        @pl.when(s < chunks)
        def _():
            load(0, s).wait()
            load(1, s).wait()
            a = jnp.dot(xa[s], pin[...], preferred_element_type=F32)
            b = jnp.dot(xg[s], pout[...], preferred_element_type=F32)
            bt = b.T
            own[s, pl.ds(0, rank), :] = bt
            own[s, pl.ds(rank, tok), :] = a
            own[s, pl.ds(rank + tok, rank), :] = bt

        cu = s - SKEW * f

        @pl.when((cu >= 0) & (cu < chunks))
        def _():
            for k in range(n):
                @pl.when(f == k)
                def _():
                    if k > 0:
                        up(k - 1, cu).wait_recv()
                    if k < n - 1:
                        at = pl.ds((k + 1) * shard, rank + tok - (k + 1) * shard)
                        x = own[cu, at, :]
                        ups[cu, at, :] = x + upr[cu, at, :] if k > 0 else x
                        up(k, cu).start()

        cd = s - SKEW * (n - 1 - f)

        @pl.when((cd >= 0) & (cd < chunks))
        def _():
            for k in range(n):
                @pl.when(f == k)
                def _():
                    if k < n - 1:
                        down(k + 1, cd).wait_recv()
                    if k > 0:
                        at = pl.ds(0, tok + k * shard)
                        x = own[cd, pl.ds(rank, tok + k * shard), :]
                        dns[cd, at, :] = x + dnr[cd, at, :] if k < n - 1 else x
                        down(k, cd).start()

        c = s - SKEW * jnp.maximum(f, n - 1 - f)

        @pl.when((c >= 0) & (c < chunks))
        def _():
            low = pl.ds(pl.multiple_of(f * shard, shard), shard)
            high = pl.ds(pl.multiple_of(tok + f * shard, shard), shard)
            tsum[pl.ds(0, tok), :] = own[c, pl.ds(rank, tok), :]
            tsum[pl.ds(tok, shard), :] = own[c, low, :]

            @pl.when(f > 0)
            def _():
                tsum[pl.ds(0, tok), :] += upr[c, pl.ds(rank, tok), :]
                tsum[pl.ds(tok, shard), :] += upr[c, low, :]

            @pl.when(f < n - 1)
            def _():
                tsum[pl.ds(0, tok), :] += dnr[c, pl.ds(0, tok), :]
                tsum[pl.ds(tok, shard), :] += dnr[c, high, :]

            full_in = tsum[pl.ds(0, tok), :]
            full_out = tsum[pl.ds(tok, shard), :]
            lane = lax.broadcasted_iota(jnp.int32, (shard, tok), 1) // tokens
            wide = jnp.concatenate(
                [jnp.where(lane == q, full_out, 0.0) for q in range(per)], axis=0
            )
            g = lax.dot_general(
                wide, full_in, (((1,), (0,)), ((), ())),
                precision=lax.Precision.HIGHEST, preferred_element_type=F32,
            )
            slot(row, sub, c)[...] = g
            for o in range(1, rows):
                across(o, c).start()
            for o in range(1, subs):
                beside(o, c).start()

        late = c - LAG

        @pl.when((late >= 0) & (late < chunks))
        def _():
            for o in range(1, rows):
                across(o, late).wait_recv()
                for p in range(1, subs):
                    onward(o, p, late).start()

        part = s - LAG

        @pl.when((part >= 0) & (part < chunks))
        def _():
            load(2, part).wait()
            hi, lo = split(st[part])
            at = pl.ds(pl.multiple_of(part * piece, piece), piece)
            shi[at, :] = hi
            slo[at, :] = lo

        return carry

    lax.fori_loop(0, chunks + SKEW * (n - 1) + LAG, step, 0)

    def settle(c, carry):
        for k in range(n):
            @pl.when(f == k)
            def _():
                if k < n - 1:
                    up(k, c).wait_send()
                if k > 0:
                    down(k, c).wait_send()

        for o in range(1, rows):
            across(o, c).wait_send()
        for o in range(1, subs):
            beside(o, c).wait()
        for o in range(1, rows):
            for p in range(1, subs):
                onward(o, p, c).wait()
        return carry

    lax.fori_loop(0, chunks, settle, 0)

    def arrange(r, carry):
        for i in range(shard):
            x = gbuf[pl.ds(r * here * shard + i, here, stride=shard), :]
            hi, lo = split(x)
            at = pl.multiple_of(r * here, here)
            glhs[pl.ds(at, here), pl.ds(i * rank, rank)] = hi
            glhs[pl.ds(total + at, here), pl.ds(i * rank, rank)] = lo
        return carry

    lax.fori_loop(0, rows * subs, arrange, 0)

    def send_scores(o, b):
        peer = lax.rem(f + o, n)
        return pltpu.make_async_remote_copy(
            sbuf.at[b, pl.ds(pl.multiple_of(peer * mine, mine), mine)], rbuf.at[o - 1, b],
            s_send.at[o - 1, b], s_recv.at[o - 1, b],
            device_id={"feat": peer}, device_id_type=MESH)

    def score(b, carry):
        at = pl.ds(pl.multiple_of(b * LANES, LANES), LANES)
        both = dot_nt(glhs[...], shi[at, :])
        cross = dot_nt(glhs[pl.ds(0, total), :], slo[at, :])
        sbuf[b] = both[:total] + (both[total:] + cross)
        for o in range(1, n):
            send_scores(o, b).start()
        return carry

    lax.fori_loop(0, blocks, score, 0)

    for b in range(blocks):
        acc = sbuf[b, pl.ds(pl.multiple_of(f * mine, mine), mine), :]
        for o in range(1, n):
            send_scores(o, b).wait_recv()
            acc = acc + rbuf[o - 1, b]
        out[:, pl.ds(b * LANES, LANES)] = acc
    for b in range(blocks):
        for o in range(1, n):
            send_scores(o, b).wait_send()


def local(n, rows, subs, acts, out_grads, proj_in, proj_out, store):
    queries, tokens, width = acts.shape
    rank = proj_in.shape[1]
    examples, feats = store.shape
    tok = LANES
    chunks = queries * tokens // tok
    shard = rank // n
    total = queries * rows * subs
    mine = total // n
    blocks = examples // LANES
    dma = pltpu.SemaphoreType.DMA
    line = pltpu.VMEM((chunks, rank + tok, rank), F32)
    vmem = pl.BlockSpec(memory_space=pltpu.VMEM)
    hbm = pl.BlockSpec(memory_space=pl.ANY)
    hops = (rows - 1) * (subs - 1)
    return pl.pallas_call(
        functools.partial(kernel, n, rows, subs, tokens),
        out_shape=jax.ShapeDtypeStruct((mine, examples), F32),
        in_specs=[hbm, hbm, vmem, vmem, hbm],
        out_specs=vmem,
        scratch_shapes=[
            pltpu.VMEM((chunks, tok, width), BF16),
            pltpu.VMEM((chunks, tok, width), BF16),
            pltpu.VMEM((chunks, examples // chunks, feats), F32),
            pltpu.VMEM((examples, feats), BF16),
            pltpu.VMEM((examples, feats), BF16),
            pltpu.VMEM((chunks, 2 * rank + tok, rank), F32),
            line, line, line, line,
            pltpu.VMEM((tok + shard, rank), F32),
            pltpu.VMEM((total * shard, rank), F32),
            pltpu.VMEM((2 * total, feats), BF16),
            pltpu.VMEM((blocks, total, LANES), F32),
            pltpu.VMEM((n - 1, blocks, mine, LANES), F32),
            dma((3, chunks)),
            dma((2, chunks)), dma((2, chunks)),
            dma((rows - 1, chunks)), dma((rows - 1, chunks)),
            dma((subs - 1, chunks)), dma((subs - 1, chunks)),
            dma((hops, chunks)), dma((hops, chunks)),
            dma((n - 1, blocks)), dma((n - 1, blocks)),
        ],
        compiler_params=pltpu.CompilerParams(
            collective_id=0, has_side_effects=True, vmem_limit_bytes=62 << 20
        ),
    )(
        acts.reshape(queries * tokens, width),
        out_grads.reshape(queries * tokens, width),
        proj_in, proj_out, store,
    )


def solution(mesh):
    n, rows, subs = (mesh.shape[a] for a in ("feat", "rows", "sub"))
    return jax.shard_map(
        functools.partial(local, n, rows, subs),
        mesh=mesh,
        in_specs=(
            P(("groups", "rows", "sub"), None, "feat"),
            P(("groups", "rows", "sub"), None, "feat"),
            P("feat", None),
            P("feat", None),
            P(("groups", "rows", "sub"), "feat"),
        ),
        out_specs=P(("groups", "feat"), ("rows", "sub")),
        check_vma=False,
    )
```

```python
import functools

import jax
import jax.numpy as jnp
from jax import lax
from jax.experimental import pallas as pl
from jax.experimental.pallas import tpu as pltpu
from jax.sharding import PartitionSpec as P

MESH = pl.DeviceIdType.MESH
LANES = 128
F32 = jnp.float32
BF16 = jnp.bfloat16
LAG = 2
AHEAD = 2
HOLD = 2
SKEW = 2


def split(x):
    hi = x.astype(BF16)
    return hi, (x - hi.astype(F32)).astype(BF16)


def dot_nt(a, b):
    return lax.dot_general(a, b, (((1,), (1,)), ((), ())), preferred_element_type=F32)


def kernel(
    n, rows, subs, tokens,
    acts, grads, pin_hbm, pout_hbm, store, out,
    pin, pout,
    xa, xg, st, shi, slo, own, ups, upr, dns, dnr, tsum, gbuf, glhs, sbuf, rbuf,
    proj_sem, load_sem, z_send, z_recv, x_send, x_recv, c_send, c_recv, f_send, f_recv, s_send, s_recv,
):
    f = lax.axis_index("feat")
    row = lax.axis_index("rows")
    sub = lax.axis_index("sub")
    chunks, tok, _ = xa.shape
    rank = pin.shape[1]
    shard = rank // n
    per = tok // tokens
    here = chunks * per
    total = here * rows * subs
    piece = store.shape[0] // chunks
    mine = total // n
    blocks = sbuf.shape[0]

    def load(kind, c):
        src, dst, size = ((acts, xa, tok), (grads, xg, tok), (store, st, piece))[kind]
        return pltpu.make_async_copy(
            src.at[pl.ds(pl.multiple_of(c * size, size), size)], dst.at[c], load_sem.at[kind, c]
        )

    proj = (
        pltpu.make_async_copy(pin_hbm, pin, proj_sem.at[0]),
        pltpu.make_async_copy(pout_hbm, pout, proj_sem.at[1]),
    )
    for kind in range(2):
        proj[kind].start()
        load(kind, 0).start()
    for c in range(1, min(AHEAD, chunks)):
        load(0, c).start()
        load(1, c).start()

    barrier = pltpu.get_barrier_semaphore()
    for o in range(1, n):
        pl.semaphore_signal(barrier, device_id={"feat": lax.rem(f + o, n)}, device_id_type=MESH)
    for o in range(1, rows):
        pl.semaphore_signal(barrier, device_id={"rows": lax.rem(row + o, rows)}, device_id_type=MESH)
    for o in range(1, subs):
        pl.semaphore_signal(barrier, device_id={"sub": lax.rem(sub + o, subs)}, device_id_type=MESH)
    pl.semaphore_wait(barrier, n + rows + subs - 3)

    def up(k, c):
        at = pl.ds((k + 1) * shard, rank + tok - (k + 1) * shard)
        return pltpu.make_async_remote_copy(
            ups.at[c, at], upr.at[c, at], z_send.at[0, c], z_recv.at[0, c],
            device_id={"feat": lax.rem(f + 1, n)}, device_id_type=MESH)

    def down(k, c):
        at = pl.ds(0, tok + k * shard)
        return pltpu.make_async_remote_copy(
            dns.at[c, at], dnr.at[c, at], z_send.at[1, c], z_recv.at[1, c],
            device_id={"feat": lax.rem(f + n - 1, n)}, device_id_type=MESH)

    def slot(r, s, c):
        size = per * shard
        return gbuf.at[pl.ds(pl.multiple_of(((r * subs + s) * chunks + c) * size, size), size)]

    def across(o, c):
        ref = slot(row, sub, c)
        return pltpu.make_async_remote_copy(
            ref, ref, x_send.at[o - 1, c], x_recv.at[o - 1, c],
            device_id={"rows": lax.rem(row + o, rows)}, device_id_type=MESH)

    def beside(o, c):
        ref = slot(row, sub, c)
        return pltpu.make_async_remote_copy(
            ref, ref, c_send.at[o - 1, c], c_recv.at[o - 1, c],
            device_id={"sub": lax.rem(sub + o, subs)}, device_id_type=MESH)

    def onward(o, p, c):
        ref = slot(lax.rem(row + rows - o, rows), sub, c)
        k = (o - 1) * (subs - 1) + p - 1
        return pltpu.make_async_remote_copy(
            ref, ref, f_send.at[k, c], f_recv.at[k, c],
            device_id={"sub": lax.rem(sub + p, subs)}, device_id_type=MESH)

    def step(s, carry):
        @pl.when(s == 0)
        def _():
            proj[0].wait()
            proj[1].wait()

        @pl.when(s + AHEAD < chunks)
        def _():
            load(0, s + AHEAD).start()
            load(1, s + AHEAD).start()

        @pl.when((s >= HOLD) & (s < HOLD + chunks))
        def _():
            load(2, s - HOLD).start()

        @pl.when(s < chunks)
        def _():
            load(0, s).wait()
            load(1, s).wait()
            a = jnp.dot(xa[s], pin[...], preferred_element_type=F32)
            b = jnp.dot(xg[s], pout[...], preferred_element_type=F32)
            bt = b.T
            own[s, pl.ds(0, rank), :] = bt
            own[s, pl.ds(rank, tok), :] = a
            own[s, pl.ds(rank + tok, rank), :] = bt

        cu = s - SKEW * f

        @pl.when((cu >= 0) & (cu < chunks))
        def _():
            for k in range(n):
                @pl.when(f == k)
                def _():
                    if k > 0:
                        up(k - 1, cu).wait_recv()
                    if k < n - 1:
                        at = pl.ds((k + 1) * shard, rank + tok - (k + 1) * shard)
                        x = own[cu, at, :]
                        ups[cu, at, :] = x + upr[cu, at, :] if k > 0 else x
                        up(k, cu).start()

        cd = s - SKEW * (n - 1 - f)

        @pl.when((cd >= 0) & (cd < chunks))
        def _():
            for k in range(n):
                @pl.when(f == k)
                def _():
                    if k < n - 1:
                        down(k + 1, cd).wait_recv()
                    if k > 0:
                        at = pl.ds(0, tok + k * shard)
                        x = own[cd, pl.ds(rank, tok + k * shard), :]
                        dns[cd, at, :] = x + dnr[cd, at, :] if k < n - 1 else x
                        down(k, cd).start()

        c = s - SKEW * jnp.maximum(f, n - 1 - f)

        @pl.when((c >= 0) & (c < chunks))
        def _():
            low = pl.ds(pl.multiple_of(f * shard, shard), shard)
            high = pl.ds(pl.multiple_of(tok + f * shard, shard), shard)
            tsum[pl.ds(0, tok), :] = own[c, pl.ds(rank, tok), :]
            tsum[pl.ds(tok, shard), :] = own[c, low, :]

            @pl.when(f > 0)
            def _():
                tsum[pl.ds(0, tok), :] += upr[c, pl.ds(rank, tok), :]
                tsum[pl.ds(tok, shard), :] += upr[c, low, :]

            @pl.when(f < n - 1)
            def _():
                tsum[pl.ds(0, tok), :] += dnr[c, pl.ds(0, tok), :]
                tsum[pl.ds(tok, shard), :] += dnr[c, high, :]

            full_in = tsum[pl.ds(0, tok), :]
            full_out = tsum[pl.ds(tok, shard), :]
            lane = lax.broadcasted_iota(jnp.int32, (shard, tok), 1) // tokens
            wide = jnp.concatenate(
                [jnp.where(lane == q, full_out, 0.0) for q in range(per)], axis=0
            )
            g = lax.dot_general(
                wide, full_in, (((1,), (0,)), ((), ())),
                precision=lax.Precision.HIGHEST, preferred_element_type=F32,
            )
            slot(row, sub, c)[...] = g
            for o in range(1, rows):
                across(o, c).start()
            for o in range(1, subs):
                beside(o, c).start()

        late = c - LAG

        @pl.when((late >= 0) & (late < chunks))
        def _():
            for o in range(1, rows):
                across(o, late).wait_recv()
                for p in range(1, subs):
                    onward(o, p, late).start()

        part = s - HOLD - LAG

        @pl.when((part >= 0) & (part < chunks))
        def _():
            load(2, part).wait()
            hi, lo = split(st[part])
            at = pl.ds(pl.multiple_of(part * piece, piece), piece)
            shi[at, :] = hi
            slo[at, :] = lo

        return carry

    lax.fori_loop(0, chunks + SKEW * (n - 1) + LAG, step, 0)

    def settle(c, carry):
        for k in range(n):
            @pl.when(f == k)
            def _():
                if k < n - 1:
                    up(k, c).wait_send()
                if k > 0:
                    down(k, c).wait_send()

        for o in range(1, rows):
            across(o, c).wait_send()
        for o in range(1, subs):
            beside(o, c).wait()
        for o in range(1, rows):
            for p in range(1, subs):
                onward(o, p, c).wait()
        return carry

    lax.fori_loop(0, chunks, settle, 0)

    def arrange(r, carry):
        for i in range(shard):
            x = gbuf[pl.ds(r * here * shard + i, here, stride=shard), :]
            hi, lo = split(x)
            at = pl.multiple_of(r * here, here)
            glhs[pl.ds(at, here), pl.ds(i * rank, rank)] = hi
            glhs[pl.ds(total + at, here), pl.ds(i * rank, rank)] = lo
        return carry

    lax.fori_loop(0, rows * subs, arrange, 0)

    def send_scores(o, b):
        peer = lax.rem(f + o, n)
        return pltpu.make_async_remote_copy(
            sbuf.at[b, pl.ds(pl.multiple_of(peer * mine, mine), mine)], rbuf.at[o - 1, b],
            s_send.at[o - 1, b], s_recv.at[o - 1, b],
            device_id={"feat": peer}, device_id_type=MESH)

    def score(b, carry):
        at = pl.ds(pl.multiple_of(b * LANES, LANES), LANES)
        both = dot_nt(glhs[...], shi[at, :])
        cross = dot_nt(glhs[pl.ds(0, total), :], slo[at, :])
        sbuf[b] = both[:total] + (both[total:] + cross)
        for o in range(1, n):
            send_scores(o, b).start()
        return carry

    lax.fori_loop(0, blocks, score, 0)

    for b in range(blocks):
        acc = sbuf[b, pl.ds(pl.multiple_of(f * mine, mine), mine), :]
        for o in range(1, n):
            send_scores(o, b).wait_recv()
            acc = acc + rbuf[o - 1, b]
        out[:, pl.ds(b * LANES, LANES)] = acc
    for b in range(blocks):
        for o in range(1, n):
            send_scores(o, b).wait_send()


def local(n, rows, subs, acts, out_grads, proj_in, proj_out, store):
    queries, tokens, width = acts.shape
    rank = proj_in.shape[1]
    examples, feats = store.shape
    tok = LANES
    chunks = queries * tokens // tok
    shard = rank // n
    total = queries * rows * subs
    mine = total // n
    blocks = examples // LANES
    dma = pltpu.SemaphoreType.DMA
    line = pltpu.VMEM((chunks, rank + tok, rank), F32)
    vmem = pl.BlockSpec(memory_space=pltpu.VMEM)
    hbm = pl.BlockSpec(memory_space=pl.ANY)
    hops = (rows - 1) * (subs - 1)
    return pl.pallas_call(
        functools.partial(kernel, n, rows, subs, tokens),
        out_shape=jax.ShapeDtypeStruct((mine, examples), F32),
        in_specs=[hbm, hbm, hbm, hbm, hbm],
        out_specs=vmem,
        scratch_shapes=[
            pltpu.VMEM(proj_in.shape, BF16),
            pltpu.VMEM(proj_out.shape, BF16),
            pltpu.VMEM((chunks, tok, width), BF16),
            pltpu.VMEM((chunks, tok, width), BF16),
            pltpu.VMEM((chunks, examples // chunks, feats), F32),
            pltpu.VMEM((examples, feats), BF16),
            pltpu.VMEM((examples, feats), BF16),
            pltpu.VMEM((chunks, 2 * rank + tok, rank), F32),
            line, line, line, line,
            pltpu.VMEM((tok + shard, rank), F32),
            pltpu.VMEM((total * shard, rank), F32),
            pltpu.VMEM((2 * total, feats), BF16),
            pltpu.VMEM((blocks, total, LANES), F32),
            pltpu.VMEM((n - 1, blocks, mine, LANES), F32),
            dma((2,)), dma((3, chunks)),
            dma((2, chunks)), dma((2, chunks)),
            dma((rows - 1, chunks)), dma((rows - 1, chunks)),
            dma((subs - 1, chunks)), dma((subs - 1, chunks)),
            dma((hops, chunks)), dma((hops, chunks)),
            dma((n - 1, blocks)), dma((n - 1, blocks)),
        ],
        compiler_params=pltpu.CompilerParams(
            collective_id=0, has_side_effects=True, vmem_limit_bytes=62 << 20
        ),
    )(
        acts.reshape(queries * tokens, width),
        out_grads.reshape(queries * tokens, width),
        proj_in, proj_out, store,
    )


def solution(mesh):
    n, rows, subs = (mesh.shape[a] for a in ("feat", "rows", "sub"))
    return jax.shard_map(
        functools.partial(local, n, rows, subs),
        mesh=mesh,
        in_specs=(
            P(("groups", "rows", "sub"), None, "feat"),
            P(("groups", "rows", "sub"), None, "feat"),
            P("feat", None),
            P("feat", None),
            P(("groups", "rows", "sub"), "feat"),
        ),
        out_specs=P(("groups", "feat"), ("rows", "sub")),
        check_vma=False,
    )
```

```python
import functools

import jax
import jax.numpy as jnp
from jax import lax
from jax.experimental import pallas as pl
from jax.experimental.pallas import tpu as pltpu
from jax.sharding import PartitionSpec as P

MESH = pl.DeviceIdType.MESH
LANES = 128
WIDE = 384
F32 = jnp.float32
BF16 = jnp.bfloat16
LAG = 2
AHEAD = 2
HOLD = 2
SKEW = 2


def split(x):
    hi = x.astype(BF16)
    return hi, (x - hi.astype(F32)).astype(BF16)


def dot_nt(a, b):
    return lax.dot_general(a, b, (((1,), (1,)), ((), ())), preferred_element_type=F32)


def kernel(
    n, rows, subs, tokens,
    acts, grads, pin_hbm, pout_hbm, store, out,
    pin, pout,
    xa, xg, st, shi, slo, own, ups, upr, dns, dnr, tsum, gbuf, glhs, sbuf, rbuf,
    proj_sem, load_sem, z_send, z_recv, x_send, x_recv, c_send, c_recv, f_send, f_recv, s_send, s_recv,
):
    f = lax.axis_index("feat")
    row = lax.axis_index("rows")
    sub = lax.axis_index("sub")
    chunks, tok, _ = xa.shape
    rank = pin.shape[1]
    shard = rank // n
    per = tok // tokens
    here = chunks * per
    total = here * rows * subs
    piece = store.shape[0] // chunks
    mine = total // n
    examples = store.shape[0]
    blocks = [(e, min(WIDE, examples - e)) for e in range(0, examples, WIDE)]

    def load(kind, c):
        src, dst, size = ((acts, xa, tok), (grads, xg, tok), (store, st, piece))[kind]
        return pltpu.make_async_copy(
            src.at[pl.ds(pl.multiple_of(c * size, size), size)], dst.at[c], load_sem.at[kind, c]
        )

    proj = (
        pltpu.make_async_copy(pin_hbm, pin, proj_sem.at[0]),
        pltpu.make_async_copy(pout_hbm, pout, proj_sem.at[1]),
    )
    for kind in range(2):
        proj[kind].start()
        load(kind, 0).start()
    for c in range(1, min(AHEAD, chunks)):
        load(0, c).start()
        load(1, c).start()

    barrier = pltpu.get_barrier_semaphore()
    for o in range(1, n):
        pl.semaphore_signal(barrier, device_id={"feat": lax.rem(f + o, n)}, device_id_type=MESH)
    for o in range(1, rows):
        pl.semaphore_signal(barrier, device_id={"rows": lax.rem(row + o, rows)}, device_id_type=MESH)
    for o in range(1, subs):
        pl.semaphore_signal(barrier, device_id={"sub": lax.rem(sub + o, subs)}, device_id_type=MESH)
    pl.semaphore_wait(barrier, n + rows + subs - 3)

    def up(k, c):
        at = pl.ds((k + 1) * shard, rank + tok - (k + 1) * shard)
        return pltpu.make_async_remote_copy(
            ups.at[c, at], upr.at[c, at], z_send.at[0, c], z_recv.at[0, c],
            device_id={"feat": lax.rem(f + 1, n)}, device_id_type=MESH)

    def down(k, c):
        at = pl.ds(0, tok + k * shard)
        return pltpu.make_async_remote_copy(
            dns.at[c, at], dnr.at[c, at], z_send.at[1, c], z_recv.at[1, c],
            device_id={"feat": lax.rem(f + n - 1, n)}, device_id_type=MESH)

    def slot(r, s, c):
        size = per * shard
        return gbuf.at[pl.ds(pl.multiple_of(((r * subs + s) * chunks + c) * size, size), size)]

    def across(o, c):
        ref = slot(row, sub, c)
        return pltpu.make_async_remote_copy(
            ref, ref, x_send.at[o - 1, c], x_recv.at[o - 1, c],
            device_id={"rows": lax.rem(row + o, rows)}, device_id_type=MESH)

    def beside(o, c):
        ref = slot(row, sub, c)
        return pltpu.make_async_remote_copy(
            ref, ref, c_send.at[o - 1, c], c_recv.at[o - 1, c],
            device_id={"sub": lax.rem(sub + o, subs)}, device_id_type=MESH)

    def onward(o, p, c):
        ref = slot(lax.rem(row + rows - o, rows), sub, c)
        k = (o - 1) * (subs - 1) + p - 1
        return pltpu.make_async_remote_copy(
            ref, ref, f_send.at[k, c], f_recv.at[k, c],
            device_id={"sub": lax.rem(sub + p, subs)}, device_id_type=MESH)

    def step(s, carry):
        @pl.when(s == 0)
        def _():
            proj[0].wait()
            proj[1].wait()

        @pl.when(s + AHEAD < chunks)
        def _():
            load(0, s + AHEAD).start()
            load(1, s + AHEAD).start()

        @pl.when((s >= HOLD) & (s < HOLD + chunks))
        def _():
            load(2, s - HOLD).start()

        @pl.when(s < chunks)
        def _():
            load(0, s).wait()
            load(1, s).wait()
            a = jnp.dot(xa[s], pin[...], preferred_element_type=F32)
            b = jnp.dot(xg[s], pout[...], preferred_element_type=F32)
            bt = b.T
            own[s, pl.ds(0, rank), :] = bt
            own[s, pl.ds(rank, tok), :] = a
            own[s, pl.ds(rank + tok, rank), :] = bt

        cu = s - SKEW * f

        @pl.when((cu >= 0) & (cu < chunks))
        def _():
            for k in range(n):
                @pl.when(f == k)
                def _():
                    if k > 0:
                        up(k - 1, cu).wait_recv()
                    if k < n - 1:
                        at = pl.ds((k + 1) * shard, rank + tok - (k + 1) * shard)
                        x = own[cu, at, :]
                        ups[cu, at, :] = x + upr[cu, at, :] if k > 0 else x
                        up(k, cu).start()

        cd = s - SKEW * (n - 1 - f)

        @pl.when((cd >= 0) & (cd < chunks))
        def _():
            for k in range(n):
                @pl.when(f == k)
                def _():
                    if k < n - 1:
                        down(k + 1, cd).wait_recv()
                    if k > 0:
                        at = pl.ds(0, tok + k * shard)
                        x = own[cd, pl.ds(rank, tok + k * shard), :]
                        dns[cd, at, :] = x + dnr[cd, at, :] if k < n - 1 else x
                        down(k, cd).start()

        c = s - SKEW * jnp.maximum(f, n - 1 - f)

        @pl.when((c >= 0) & (c < chunks))
        def _():
            low = pl.ds(pl.multiple_of(f * shard, shard), shard)
            high = pl.ds(pl.multiple_of(tok + f * shard, shard), shard)
            tsum[pl.ds(0, tok), :] = own[c, pl.ds(rank, tok), :]
            tsum[pl.ds(tok, shard), :] = own[c, low, :]

            @pl.when(f > 0)
            def _():
                tsum[pl.ds(0, tok), :] += upr[c, pl.ds(rank, tok), :]
                tsum[pl.ds(tok, shard), :] += upr[c, low, :]

            @pl.when(f < n - 1)
            def _():
                tsum[pl.ds(0, tok), :] += dnr[c, pl.ds(0, tok), :]
                tsum[pl.ds(tok, shard), :] += dnr[c, high, :]

            full_in = tsum[pl.ds(0, tok), :]
            full_out = tsum[pl.ds(tok, shard), :]
            lane = lax.broadcasted_iota(jnp.int32, (shard, tok), 1) // tokens
            wide = jnp.concatenate(
                [jnp.where(lane == q, full_out, 0.0) for q in range(per)], axis=0
            )
            g = lax.dot_general(
                wide, full_in, (((1,), (0,)), ((), ())),
                precision=lax.Precision.HIGHEST, preferred_element_type=F32,
            )
            slot(row, sub, c)[...] = g
            for o in range(1, rows):
                across(o, c).start()
            for o in range(1, subs):
                beside(o, c).start()

        late = c - LAG

        @pl.when((late >= 0) & (late < chunks))
        def _():
            for o in range(1, rows):
                across(o, late).wait_recv()
                for p in range(1, subs):
                    onward(o, p, late).start()

        part = s - HOLD - LAG

        @pl.when((part >= 0) & (part < chunks))
        def _():
            load(2, part).wait()
            hi, lo = split(st[part])
            at = pl.ds(pl.multiple_of(part * piece, piece), piece)
            shi[at, :] = hi
            slo[at, :] = lo

        return carry

    lax.fori_loop(0, chunks + SKEW * (n - 1) + LAG, step, 0)

    def settle(c, carry):
        for k in range(n):
            @pl.when(f == k)
            def _():
                if k < n - 1:
                    up(k, c).wait_send()
                if k > 0:
                    down(k, c).wait_send()

        for o in range(1, rows):
            across(o, c).wait_send()
        for o in range(1, subs):
            beside(o, c).wait()
        for o in range(1, rows):
            for p in range(1, subs):
                onward(o, p, c).wait()
        return carry

    lax.fori_loop(0, chunks, settle, 0)

    def arrange(r, carry):
        for i in range(shard):
            x = gbuf[pl.ds(r * here * shard + i, here, stride=shard), :]
            hi, lo = split(x)
            at = pl.multiple_of(r * here, here)
            glhs[pl.ds(at, here), pl.ds(i * rank, rank)] = hi
            glhs[pl.ds(total + at, here), pl.ds(i * rank, rank)] = lo
        return carry

    lax.fori_loop(0, rows * subs, arrange, 0)

    def send_scores(o, b):
        peer = lax.rem(f + o, n)
        cols = pl.ds(*blocks[b])
        return pltpu.make_async_remote_copy(
            sbuf.at[pl.ds(pl.multiple_of(peer * mine, mine), mine), cols],
            rbuf.at[o - 1, pl.ds(0, mine), cols],
            s_send.at[o - 1, b], s_recv.at[o - 1, b],
            device_id={"feat": peer}, device_id_type=MESH)

    for b in range(len(blocks)):
        at = pl.ds(*blocks[b])
        both = dot_nt(glhs[...], shi[at, :])
        cross = dot_nt(glhs[pl.ds(0, total), :], slo[at, :])
        sbuf[:, at] = both[:total] + (both[total:] + cross)
        for o in range(1, n):
            send_scores(o, b).start()

    for b in range(len(blocks)):
        cols = pl.ds(*blocks[b])
        acc = sbuf[pl.ds(pl.multiple_of(f * mine, mine), mine), cols]
        for o in range(1, n):
            send_scores(o, b).wait_recv()
            acc = acc + rbuf[o - 1, :, cols]
        out[:, cols] = acc
    for b in range(len(blocks)):
        for o in range(1, n):
            send_scores(o, b).wait_send()


def local(n, rows, subs, acts, out_grads, proj_in, proj_out, store):
    queries, tokens, width = acts.shape
    rank = proj_in.shape[1]
    examples, feats = store.shape
    tok = LANES
    chunks = queries * tokens // tok
    shard = rank // n
    total = queries * rows * subs
    mine = total // n
    blocks = pl.cdiv(examples, WIDE)
    dma = pltpu.SemaphoreType.DMA
    line = pltpu.VMEM((chunks, rank + tok, rank), F32)
    vmem = pl.BlockSpec(memory_space=pltpu.VMEM)
    hbm = pl.BlockSpec(memory_space=pl.ANY)
    hops = (rows - 1) * (subs - 1)
    return pl.pallas_call(
        functools.partial(kernel, n, rows, subs, tokens),
        out_shape=jax.ShapeDtypeStruct((mine, examples), F32),
        in_specs=[hbm, hbm, hbm, hbm, hbm],
        out_specs=vmem,
        scratch_shapes=[
            pltpu.VMEM(proj_in.shape, BF16),
            pltpu.VMEM(proj_out.shape, BF16),
            pltpu.VMEM((chunks, tok, width), BF16),
            pltpu.VMEM((chunks, tok, width), BF16),
            pltpu.VMEM((chunks, examples // chunks, feats), F32),
            pltpu.VMEM((examples, feats), BF16),
            pltpu.VMEM((examples, feats), BF16),
            pltpu.VMEM((chunks, 2 * rank + tok, rank), F32),
            line, line, line, line,
            pltpu.VMEM((tok + shard, rank), F32),
            pltpu.VMEM((total * shard, rank), F32),
            pltpu.VMEM((2 * total, feats), BF16),
            pltpu.VMEM((total, examples), F32),
            pltpu.VMEM((n - 1, mine, examples), F32),
            dma((2,)), dma((3, chunks)),
            dma((2, chunks)), dma((2, chunks)),
            dma((rows - 1, chunks)), dma((rows - 1, chunks)),
            dma((subs - 1, chunks)), dma((subs - 1, chunks)),
            dma((hops, chunks)), dma((hops, chunks)),
            dma((n - 1, blocks)), dma((n - 1, blocks)),
        ],
        compiler_params=pltpu.CompilerParams(
            collective_id=0, has_side_effects=True, vmem_limit_bytes=62 << 20
        ),
    )(
        acts.reshape(queries * tokens, width),
        out_grads.reshape(queries * tokens, width),
        proj_in, proj_out, store,
    )


def solution(mesh):
    n, rows, subs = (mesh.shape[a] for a in ("feat", "rows", "sub"))
    return jax.shard_map(
        functools.partial(local, n, rows, subs),
        mesh=mesh,
        in_specs=(
            P(("groups", "rows", "sub"), None, "feat"),
            P(("groups", "rows", "sub"), None, "feat"),
            P("feat", None),
            P("feat", None),
            P(("groups", "rows", "sub"), "feat"),
        ),
        out_specs=P(("groups", "feat"), ("rows", "sub")),
        check_vma=False,
    )
```
